128 devices in a mesh: row: 16 (over x, y_lo, core), col: 8 (over z, y_hi).
Axes of the slice: x: 4, y: 4 (y_hi: 2, y_lo: 2; y = y_hi * 2 + y_lo), z: 4, core: 2. Of those that a mesh axis runs over, the one named last changes fastest.
Arguments:
- x_blocks: bfloat16 [256, 16, 2, 128, 128], P('row', 'col'), may hold values from -1.796875 to 1.796875
- x_columns: int32 [256, 16, 2], P('row', 'col'), may hold values from 0 to 95, as said below
- kept_columns: int32 [1536, 16], P('row', 'col'), may hold values from 0 to 191, as said below
Outputs:
- result_blocks: float32 [1536, 16, 128, 128], P('row', 'col')
The draws below stay inside these ranges and needn't reach their ends.
Inputs may be any that keep to these rules, and one draw needn't show every extreme that they name: `x_columns`: the 2 entries of one block row and one group are distinct. `kept_columns`: the 2 entries of one result block row within one column panel are distinct.
All inputs are finite; a program needn't handle non-finite values.
Results may differ from the reference program's by a relative error of at most 0.0003.
Values may be sent and summed in bfloat16 or wider, within the bound.
A program may use at most 320 MiB of HBM per device.

```python
import jax
import jax.numpy as jnp
from jax import lax

BS = 128
GW = 96
E = 2
F = 2
BROWS = 256
GROUPS = 16
GPANEL = 2
N_COL = 8


def shared_columns(key):
    col_key = jax.random.fold_in(key, 31)
    scores = jax.random.randint(col_key, (BROWS, GROUPS, GW), 0, 2 ** 16) * GW
    scores = scores + lax.broadcasted_iota(jnp.int32, (BROWS, GROUPS, GW), 2)
    _, picked = lax.top_k(scores, E)
    return picked.astype(jnp.int32)


def draw_x_columns(key, part):
    return shared_columns(key)


def draw_kept_columns(key, part):
    columns = shared_columns(key)
    rows_all = GROUPS * GW
    local_pos = lax.broadcasted_iota(jnp.int32, (GW,), 0)
    by_group = columns.transpose(1, 0, 2)
    cover = jnp.any(by_group[:, None, :, :] == local_pos[None, :, None, None], axis=3).reshape(rows_all, BROWS)
    row_scores = jax.random.randint(jax.random.fold_in(key, 32), (rows_all, N_COL, BROWS), 0, 2 ** 14) * BROWS
    row_scores = row_scores + lax.broadcasted_iota(jnp.int32, (rows_all, N_COL, BROWS), 2)
    masked = jnp.where(cover[:, None, :], row_scores, -1)
    best, chosen = lax.top_k(masked, 1)
    has_cover = best[:, :, 0] >= 0
    picked_rows = jnp.take(columns, chosen[:, :, 0].astype(jnp.int32), axis=0)
    picked_rows = picked_rows.reshape(rows_all, N_COL, N_COL, GPANEL, E)
    same_panel = lax.broadcasted_iota(jnp.int32, (N_COL, N_COL), 0) == lax.broadcasted_iota(jnp.int32, (N_COL, N_COL), 1)
    in_panel = jnp.sum(jnp.where(same_panel[None, :, :, None, None], picked_rows, 0), axis=2)
    group_base = lax.broadcasted_iota(jnp.int32, (GPANEL,), 0) * GW
    candidates = (in_panel + group_base[None, None, :, None]).reshape(rows_all, N_COL, GPANEL * E)
    pick_scores = jax.random.randint(jax.random.fold_in(key, 33), (rows_all, N_COL, GPANEL * E), 0, 2 ** 16) * (GPANEL * E)
    pick_scores = pick_scores + lax.broadcasted_iota(jnp.int32, (rows_all, N_COL, GPANEL * E), 2)
    _, order = lax.top_k(pick_scores, F)
    from_row = jnp.take_along_axis(candidates, order.astype(jnp.int32), axis=2)
    start = jax.random.randint(jax.random.fold_in(key, 34), (rows_all, N_COL, 1), 0, GPANEL * GW)
    spare = (start + lax.broadcasted_iota(jnp.int32, (1, 1, F), 2)) % (GPANEL * GW)
    kept = jnp.where(has_cover[:, :, None], from_row, spare)
    return kept.reshape(rows_all, N_COL * F).astype(jnp.int32)


def block_scale(stream_key, extent, cuts, least, high):
    def one(axis_at, blocks):
        heights = jax.random.uniform(jax.random.fold_in(jax.random.fold_in(stream_key, 6), axis_at), (blocks,), jnp.float32, least / len(cuts), high / len(cuts))
        return jnp.repeat(jnp.exp(heights), extent[axis_at] // blocks).reshape((-1,) + (1,) * (len(extent) - axis_at - 1))

    factor_of = one(*cuts[0])
    for cut in cuts[1:]:
        factor_of = factor_of * one(*cut)
    return factor_of


def bell_draw(key, extent, width, reach, cuts=(), held_as=jnp.bfloat16):
    values = jax.random.normal(key, extent, jnp.float32) * width
    if len(cuts) > 0:
        values = block_scale(key, extent, cuts, -0.22, 0.18) * values
    return jnp.clip(values, min=-reach, max=reach).astype(held_as)


def setup_inputs(seed: int = 0) -> dict:
    splits = jax.random.split(jax.random.key(seed), 4)
    return {
        "x_blocks": bell_draw(splits[0], (BROWS, GROUPS, E, BS, BS), 0.3, 1.796875, ((0, 16), (1, 8))),
        "x_columns": draw_x_columns(jax.random.fold_in(splits[3], 71), 0),
        "kept_columns": draw_kept_columns(jax.random.fold_in(splits[3], 71), 0),
    }


def reference(x_blocks, x_columns, kept_columns):
    brows, groups, slots = x_columns.shape
    block_size = x_blocks.shape[-1]
    per_row = N_COL * F
    gpanel = groups // N_COL
    block_count = groups * slots
    group_of = jnp.repeat(jnp.arange(groups, dtype=jnp.int32), slots)
    total_slots = groups * GW * per_row
    panel_of = group_of // gpanel

    def scan_step(accumulated, row_pair):
        row_values, row_cols = row_pair
        flat_v = row_values.reshape(block_count, block_size, block_size).astype(jnp.float32)
        flat_c = row_cols.reshape(block_count).astype(jnp.int32)
        products = jnp.einsum("ati,btj->abij", flat_v, flat_v)
        out_row = group_of * GW + flat_c
        in_panel = (group_of % gpanel) * GW + flat_c
        kept_rows = jnp.take(kept_columns, out_row, axis=0).reshape(block_count, N_COL, F)
        chosen = kept_rows[:, panel_of, :]
        matches = chosen == in_panel[None, :, None]
        is_hit = jnp.any(matches, axis=2)
        slot_pick = jnp.sum(jnp.where(matches, jnp.arange(F, dtype=jnp.int32)[None, None, :], 0), axis=2).astype(jnp.int32)
        target = jnp.where(is_hit, (out_row[:, None] * N_COL + panel_of[None, :]) * F + slot_pick, total_slots).astype(jnp.int32)
        accumulated = accumulated.at[target.reshape(-1)].add(products.reshape(-1, block_size, block_size), mode="drop")
        return accumulated, None

    zero_sums = jnp.zeros((total_slots, block_size, block_size), jnp.float32)
    accumulated, _ = lax.scan(scan_step, zero_sums, (x_blocks, x_columns))
    return accumulated.reshape(groups * GW, per_row, block_size, block_size)
```

```python
import functools

import jax
import jax.numpy as jnp
from jax import lax
from jax.experimental import pallas as pl
from jax.experimental.pallas import tpu as pltpu
from jax.sharding import PartitionSpec as P

K_STEP = 32


def match_tables(a_cols, b_cols, kept_columns):
    k_count, slots = a_cols.shape
    width_g = kept_columns.shape[0]
    panel_pos = (lax.broadcasted_iota(jnp.int32, b_cols.shape, 1) * width_g + b_cols).reshape(k_count, -1)
    onehot = a_cols[:, :, None] == lax.broadcasted_iota(jnp.int32, (1, 1, width_g), 2)
    kept_here = jnp.sum(jnp.where(onehot[:, :, :, None], kept_columns[None, None, :, :], 0), axis=2)
    matches = kept_here[:, :, :, None] == panel_pos[:, None, None, :]
    f_index = lax.broadcasted_iota(jnp.int32, matches.shape, 3)
    picked = jnp.sum(jnp.where(matches, f_index, 0), axis=3)
    sel = jnp.where(jnp.any(matches, axis=3), picked, -1)
    return a_cols.reshape(-1).astype(jnp.int32), sel.reshape(-1).astype(jnp.int32)


def products_kernel(rows_ref, sel_ref, a_ref, b_ref, out_ref):
    step = pl.program_id(0)
    k_step = a_ref.shape[0]
    slots = a_ref.shape[1]
    kept = out_ref.shape[1]

    @pl.when(step == 0)
    def _():
        out_ref[...] = jnp.zeros_like(out_ref)

    def body(kk, carry):
        k = step * k_step + kk
        for e in range(slots):
            row = rows_ref[k * slots + e]
            a = a_ref[kk, e]
            for s in range(kept):
                f = sel_ref[(k * slots + e) * kept + s]

                @pl.when(f >= 0)
                def _():
                    b = b_ref[kk, f]
                    out_ref[row, s] += lax.dot_general(
                        a, b, (((0,), (0,)), ((), ())), preferred_element_type=jnp.float32
                    )

        return carry

    lax.fori_loop(0, k_step, body, 0)


def block_products(a_values, b_values, rows, sel, width_g, kept):
    k_count, slots, bs, _ = a_values.shape
    b_flat = b_values.reshape(k_count, -1, bs, bs)
    nb = b_flat.shape[1]
    steps = k_count // K_STEP
    return pl.pallas_call(
        products_kernel,
        out_shape=jax.ShapeDtypeStruct((width_g, kept, bs, bs), jnp.float32),
        grid_spec=pltpu.PrefetchScalarGridSpec(
            num_scalar_prefetch=2,
            grid=(steps,),
            in_specs=[
                pl.BlockSpec((K_STEP, slots, bs, bs), lambda i, r, s: (i, 0, 0, 0)),
                pl.BlockSpec((K_STEP, nb, bs, bs), lambda i, r, s: (i, 0, 0, 0)),
            ],
            out_specs=pl.BlockSpec(
                (width_g, kept, bs, bs), lambda i, r, s: (0, 0, 0, 0), pipeline_mode=pl.Buffered(1)
            ),
        ),
        compiler_params=pltpu.CompilerParams(
            dimension_semantics=("arbitrary",), vmem_limit_bytes=60 * 1024 * 1024
        ),
        cost_estimate=pl.CostEstimate(
            flops=2 * k_count * slots * kept * bs * bs * bs,
            bytes_accessed=(a_values.size + b_values.size) * 2 + width_g * kept * bs * bs * 4,
            transcendentals=0,
        ),
    )(rows, sel, a_values, b_flat)


def on_device(x_blocks, x_columns, kept_columns):
    rows_here = x_blocks.shape[0]
    slot_count = x_blocks.shape[2]
    block_size = x_blocks.shape[-1]
    width_g = kept_columns.shape[0]
    kept = kept_columns.shape[1]
    n_row = lax.axis_size("row")
    n_col = lax.axis_size("col")
    col_tags = x_columns.astype(jnp.bfloat16)
    relaid = (
        lax.all_to_all(x_blocks, "col", split_axis=0, concat_axis=1, tiled=True),
        lax.all_to_all(col_tags, "col", split_axis=0, concat_axis=1, tiled=True),
    )
    relaid = (
        lax.all_to_all(relaid[0], "row", split_axis=1, concat_axis=0, tiled=True),
        lax.all_to_all(relaid[1], "row", split_axis=1, concat_axis=0, tiled=True),
    )
    gathered = (
        lax.all_gather(relaid[0][:, 0], "col", axis=0, tiled=True),
        lax.all_gather(relaid[1][:, 0], "col", axis=0, tiled=True),
    )
    sub_rows = rows_here // n_col
    a_values = gathered[0].reshape(n_col, n_row, sub_rows, slot_count, block_size, block_size)
    a_values = a_values.transpose(1, 0, 2, 3, 4, 5).reshape(
        n_row * rows_here, slot_count, block_size, block_size
    )
    a_cols = gathered[1].reshape(n_col, n_row, sub_rows, slot_count).transpose(1, 0, 2, 3)
    a_cols = a_cols.reshape(n_row * rows_here, slot_count).astype(jnp.int32)
    b_values = lax.all_gather(x_blocks, "row", axis=0, tiled=True)
    b_tags = lax.all_gather(col_tags, "row", axis=0, tiled=True)
    rows, sel = match_tables(a_cols, b_tags.astype(jnp.int32), kept_columns)
    return block_products(a_values, b_values, rows, sel, width_g, kept)


def solution(mesh):
    placed = (P("row", "col", None, None, None), P("row", "col", None), P("row", "col"))
    return jax.shard_map(
        on_device,
        mesh=mesh,
        in_specs=placed,
        out_specs=P("row", "col", None, None),
        check_vma=False,
    )
```
